32 devices in a mesh: dp: 4 (over y, x), mdl: 4 (over z), emb: 2 (over core).
Axes of the slice: x: 2, y: 2, z: 4, core: 2. Of those that a mesh axis runs over, the one named last changes fastest.
Arguments:
- inputs: float32 [4096, 1152], P(('dp', 'mdl'), 'emb'), may hold values from -40 to 40
- norm1_gain: float32 [1152], P('emb'), may hold values from 0.1 to 1.9
- norm1_shift: float32 [1152], P('emb'), may hold values from -3 to 3
- qkv_weight: bfloat16 [1152, 3456], P('emb', 'mdl'), may hold values from -0.55 to 0.55
- query_bias: float32 [1152], P('mdl'), may hold values from -3 to 3
- value_bias: float32 [1152], P('mdl'), may hold values from -3 to 3
- out_weight: bfloat16 [1152, 1152], P('mdl', 'emb'), may hold values from -1.5 to 1.5
- out_bias: float32 [1152], P('emb'), may hold values from -3 to 3
- norm2_gain: float32 [1152], P('emb'), may hold values from 0.1 to 1.9
- norm2_shift: float32 [1152], P('emb'), may hold values from -3 to 3
- fc1_weight: bfloat16 [1152, 4304], P('emb', 'mdl'), may hold values from -0.1875 to 0.1875
- fc1_bias: float32 [4304], P('mdl'), may hold values from -3 to 3
- fc2_weight: bfloat16 [4304, 1152], P('mdl', 'emb'), may hold values from -0.09375 to 0.09375
- fc2_bias: float32 [1152], P('emb'), may hold values from -3 to 3
- cotangent: float32 [4096, 1152], P(('dp', 'mdl'), 'emb'), may hold values from -6 to 6
Outputs:
- outputs: float32 [4096, 1152], P(('dp', 'mdl'), 'emb')
- input_grad: float32 [4096, 1152], P(('dp', 'mdl'), 'emb')
- norm1_gain_grad: float32 [1152], P('emb')
- norm1_shift_grad: float32 [1152], P('emb')
- qkv_weight_grad: float32 [1152, 3456], P('emb', 'mdl')
- query_bias_grad: float32 [1152], P('mdl')
- value_bias_grad: float32 [1152], P('mdl')
- out_weight_grad: float32 [1152, 1152], P('mdl', 'emb')
- out_bias_grad: float32 [1152], P('emb')
- norm2_gain_grad: float32 [1152], P('emb')
- norm2_shift_grad: float32 [1152], P('emb')
- fc1_weight_grad: float32 [1152, 4304], P('emb', 'mdl')
- fc1_bias_grad: float32 [4304], P('mdl')
- fc2_weight_grad: float32 [4304, 1152], P('mdl', 'emb')
- fc2_bias_grad: float32 [1152], P('emb')
The draws below stay inside these ranges and needn't reach their ends.
All inputs are finite; a program needn't handle non-finite values.
Results may differ from the reference program's by a relative error of at most 0.015.
The reference program's roundings to bfloat16 on the way count: a program that leaves them out, or rounds other values in their place, can miss the bound.
Values may be sent and summed in bfloat16 or wider, within the bound.
No kernel may reach another device: no remote copies, remote signals or barrier semaphores. Data moves between devices by JAX's collectives and lax.ppermute only.
A program may use at most 128 MiB of HBM per device.

```python
import math
import jax
import jax.numpy as jnp
from jax import lax

D = 1152
FF = 4304
HEADS = 16
HD = 72
SEQ = 256
IMG_DEV = 4
TOKENS = 4096


def draw_inputs(key, part):
    row_key, col_key, base_key = jax.random.split(key, 3)
    row_scale = 0.3 * jnp.exp(jax.random.uniform(row_key, (TOKENS, 1), minval=0.0, maxval=math.log(10.0)))
    col_scale = jnp.exp(jax.random.uniform(col_key, (1, D), minval=-0.5 * math.log(10.0), maxval=0.5 * math.log(10.0)))
    base = jnp.clip(jax.random.normal(base_key, (TOKENS, D)), -4.0, 4.0)
    return (base * row_scale * col_scale).astype(jnp.float32)


def draw_qkv_weight(key, part):
    base_key = jax.random.fold_in(key, 0)
    base = jnp.clip(jax.random.normal(base_key, (D, HEADS, 3, HD)), -4.0, 4.0)
    values = base * (1.0 / math.sqrt(D))
    return values.reshape(D, 3 * D).astype(jnp.bfloat16)


def shard_levels(key, dims, shards, low, high):
    def one(position, parts):
        steps = jax.random.uniform(jax.random.fold_in(jax.random.fold_in(key, 6), position), (parts,), jnp.float32, low / len(shards), high / len(shards))
        return jnp.repeat(jnp.exp(steps), dims[position] // parts).reshape((-1,) + (1,) * (len(dims) - position - 1))

    gain = one(*shards[0])
    for cut in shards[1:]:
        gain = gain * one(*cut)
    return gain


def gaussian(key, shape, scale, most, cuts=(), kind=jnp.bfloat16):
    drawn = scale * jax.random.normal(key, shape, jnp.float32)
    if cuts:
        drawn = drawn * shard_levels(key, shape, cuts, -0.22, 0.18)
    return jnp.clip(drawn, -most, most).astype(kind)


def setup_inputs(seed: int = 0) -> dict:
    streams_of = jax.random.split(jax.random.key(seed), 16)
    inputs = draw_inputs(jax.random.fold_in(streams_of[15], 71), 0)
    norm1_gain = jnp.clip(1.0 + 0.18 * jax.random.normal(streams_of[1], (D,), jnp.float32), 0.1, 1.9)
    norm1_shift = gaussian(streams_of[2], (D,), 0.5, 3.0, ((0, 2),), jnp.float32)
    qkv_weight = draw_qkv_weight(jax.random.fold_in(streams_of[15], 71), 0)
    query_bias = gaussian(streams_of[4], (D,), 0.5, 3.0, ((0, 4),), jnp.float32)
    value_bias = gaussian(streams_of[5], (D,), 0.5, 3.0, ((0, 4),), jnp.float32)
    out_weight = gaussian(streams_of[6], (D, D), (D // 64) ** -0.5, 1.5, ((0, 4), (1, 2)))
    out_bias = gaussian(streams_of[7], (D,), 0.5, 3.0, ((0, 2),), jnp.float32)
    norm2_gain = jnp.clip(1.0 + 0.18 * jax.random.normal(streams_of[8], (D,), jnp.float32), 0.1, 1.9)
    norm2_shift = gaussian(streams_of[9], (D,), 0.5, 3.0, ((0, 2),), jnp.float32)
    fc1_weight = gaussian(streams_of[10], (D, FF), D ** -0.5, 0.1875, ((0, 2), (1, 4)))
    fc1_bias = gaussian(streams_of[11], (FF,), 0.5, 3.0, ((0, 4),), jnp.float32)
    fc2_weight = gaussian(streams_of[12], (FF, D), FF ** -0.5, 0.09375, ((0, 4), (1, 2)))
    fc2_bias = gaussian(streams_of[13], (D,), 0.5, 3.0, ((0, 2),), jnp.float32)
    cotangent = gaussian(streams_of[14], (TOKENS, D), 1.0, 6.0, ((0, 16), (1, 2)), jnp.float32)
    return dict(inputs=inputs, norm1_gain=norm1_gain, norm1_shift=norm1_shift, qkv_weight=qkv_weight, query_bias=query_bias, value_bias=value_bias, out_weight=out_weight, out_bias=out_bias, norm2_gain=norm2_gain, norm2_shift=norm2_shift, fc1_weight=fc1_weight, fc1_bias=fc1_bias, fc2_weight=fc2_weight, fc2_bias=fc2_bias, cotangent=cotangent)


EPS = 1e-06
CUBIC = 0.044715
ROOT = math.sqrt(2.0 / math.pi)

def matmul(left, right):
    return jnp.dot(left, right, preferred_element_type=jnp.float32)

def outer_sum(left, right):
    return lax.dot_general(left, right, (((0,), (0,)), ((), ())), preferred_element_type=jnp.float32)

def times_transpose(left, right):
    return lax.dot_general(left, right, (((1,), (1,)), ((), ())), preferred_element_type=jnp.float32)

def rounded(values):
    return lax.optimization_barrier(values.astype(jnp.bfloat16)).astype(jnp.float32)

def norm_rows(inputs, gain_row, shift_row):
    average = lax.optimization_barrier(jnp.mean(inputs, axis=1, keepdims=True))
    variance = lax.optimization_barrier(jnp.mean(inputs * inputs, axis=1, keepdims=True)) - average * average
    inverse = lax.rsqrt(variance + EPS)
    centered = (inputs - average) * inverse
    return (centered, inverse, (centered * gain_row + shift_row).astype(jnp.bfloat16))

def norm_back(normed_grad, centered, inverse, gain_row):
    scaled = normed_grad * gain_row
    first = lax.optimization_barrier(jnp.mean(scaled, axis=1, keepdims=True))
    second = lax.optimization_barrier(jnp.mean(scaled * centered, axis=1, keepdims=True))
    return inverse * (scaled - first - centered * second)

def gelu_parts(pre_act):
    inner = ROOT * (pre_act + CUBIC * pre_act * pre_act * pre_act)
    hyper = jnp.tanh(inner)
    values = 0.5 * pre_act * (1.0 + hyper)
    slope = 0.5 * (1.0 + hyper) + 0.5 * pre_act * (1.0 - hyper * hyper) * ROOT * (1.0 + 3.0 * CUBIC * pre_act * pre_act)
    return (values, slope)

def attend(qkv):
    queries = qkv[:, :, :, 0].astype(jnp.float32)
    key_rows = qkv[:, :, :, 1].astype(jnp.float32)
    value_rows = qkv[:, :, :, 2].astype(jnp.float32)
    factor = 1.0 / math.sqrt(HD)
    scores = jnp.einsum('bqhd,bkhd->bhqk', queries, key_rows) * factor
    highest = lax.optimization_barrier(jnp.max(scores, axis=3, keepdims=True))
    log_total = highest + jnp.log(lax.optimization_barrier(jnp.sum(jnp.exp(scores - highest), axis=3, keepdims=True)))
    chances = rounded(jnp.exp(scores - log_total))
    attended = jnp.einsum('bhqk,bkhd->bqhd', chances, value_rows).astype(jnp.bfloat16)
    return (attended, log_total)

def attend_back(qkv, attended, log_total, attended_grad):
    queries = qkv[:, :, :, 0].astype(jnp.float32)
    key_rows = qkv[:, :, :, 1].astype(jnp.float32)
    value_rows = qkv[:, :, :, 2].astype(jnp.float32)
    factor = 1.0 / math.sqrt(HD)
    scores = jnp.einsum('bqhd,bkhd->bhqk', queries, key_rows) * factor
    chances = jnp.exp(scores - log_total)
    grad_full = attended_grad.astype(jnp.float32)
    value_grad = jnp.einsum('bhqk,bqhd->bkhd', rounded(chances), grad_full).astype(jnp.bfloat16)
    chance_grad = jnp.einsum('bqhd,bkhd->bhqk', grad_full, value_rows)
    row_dot = jnp.einsum('bqhd,bqhd->bhq', grad_full, attended.astype(jnp.float32))[..., None]
    score_grad = rounded(chances * (chance_grad - row_dot))
    query_grad = (jnp.einsum('bhqk,bkhd->bqhd', score_grad, key_rows) * factor).astype(jnp.bfloat16)
    key_grad = (jnp.einsum('bhqk,bqhd->bkhd', score_grad, queries) * factor).astype(jnp.bfloat16)
    return jnp.stack([query_grad, key_grad, value_grad], axis=3)

def reference(inputs, norm1_gain, norm1_shift, qkv_weight, query_bias, value_bias, out_weight, out_bias, norm2_gain, norm2_shift, fc1_weight, fc1_bias, fc2_weight, fc2_bias, cotangent):
    block_rows = IMG_DEV * SEQ
    blocks = TOKENS // block_rows
    bias_full = jnp.stack([query_bias.reshape(HEADS, HD), jnp.zeros((HEADS, HD), jnp.float32), value_bias.reshape(HEADS, HD)], axis=1)

    def step(carry, pair):
        block_in, block_cot = pair
        centered1, inverse1, normed1 = norm_rows(block_in, norm1_gain, norm1_shift)
        mixed = matmul(normed1, qkv_weight).reshape(IMG_DEV, SEQ, HEADS, 3, HD) + bias_full
        qkv = mixed.astype(jnp.bfloat16)
        attended, log_total = attend(qkv)
        attended_flat = attended.reshape(block_rows, D)
        middle = block_in + matmul(attended_flat, out_weight) + out_bias
        centered2, inverse2, normed2 = norm_rows(middle, norm2_gain, norm2_shift)
        pre_act = matmul(normed2, fc1_weight) + fc1_bias
        act_values, slope = gelu_parts(pre_act)
        activation = act_values.astype(jnp.bfloat16)
        outputs = middle + matmul(activation, fc2_weight) + fc2_bias
        cot_rounded = block_cot.astype(jnp.bfloat16)
        fc2_weight_grad = outer_sum(activation, cot_rounded)
        fc2_bias_grad = lax.optimization_barrier(jnp.sum(block_cot, axis=0))
        pre_grad = (times_transpose(cot_rounded, fc2_weight) * slope).astype(jnp.bfloat16)
        fc1_weight_grad = outer_sum(normed2, pre_grad)
        fc1_bias_grad = lax.optimization_barrier(jnp.sum(pre_grad.astype(jnp.float32), axis=0))
        normed2_grad = times_transpose(pre_grad, fc1_weight)
        norm2_gain_grad = lax.optimization_barrier(jnp.sum(normed2_grad * centered2, axis=0))
        norm2_shift_grad = lax.optimization_barrier(jnp.sum(normed2_grad, axis=0))
        middle_grad = block_cot + norm_back(normed2_grad, centered2, inverse2, norm2_gain)
        out_bias_grad = lax.optimization_barrier(jnp.sum(middle_grad, axis=0))
        mid_rounded = middle_grad.astype(jnp.bfloat16)
        out_weight_grad = outer_sum(attended_flat, mid_rounded)
        attended_grad = times_transpose(mid_rounded, out_weight).astype(jnp.bfloat16).reshape(IMG_DEV, SEQ, HEADS, HD)
        qkv_grad = attend_back(qkv, attended, log_total, attended_grad)
        qkv_flat = qkv_grad.reshape(block_rows, 3 * D)
        qkv_weight_grad = outer_sum(normed1, qkv_flat)
        column_sums = lax.optimization_barrier(jnp.sum(qkv_flat.astype(jnp.float32), axis=0)).reshape(HEADS, 3, HD)
        query_bias_grad = column_sums[:, 0].reshape(D)
        value_bias_grad = column_sums[:, 2].reshape(D)
        normed1_grad = times_transpose(qkv_flat, qkv_weight)
        norm1_gain_grad = lax.optimization_barrier(jnp.sum(normed1_grad * centered1, axis=0))
        norm1_shift_grad = lax.optimization_barrier(jnp.sum(normed1_grad, axis=0))
        input_grad = middle_grad + norm_back(normed1_grad, centered1, inverse1, norm1_gain)
        grads = (norm1_gain_grad, norm1_shift_grad, qkv_weight_grad, query_bias_grad, value_bias_grad, out_weight_grad, out_bias_grad, norm2_gain_grad, norm2_shift_grad, fc1_weight_grad, fc1_bias_grad, fc2_weight_grad, fc2_bias_grad)
        updated = tuple((old + new for old, new in zip(carry, grads)))
        return (updated, (outputs, input_grad))
    shapes = [(D,), (D,), (D, 3 * D), (D,), (D,), (D, D), (D,), (D,), (D,), (D, FF), (FF,), (FF, D), (D,)]
    start = tuple((jnp.zeros(shape, jnp.float32) for shape in shapes))
    stacked = (inputs.reshape(blocks, block_rows, D), cotangent.reshape(blocks, block_rows, D))
    totals, (outputs, input_grad) = lax.scan(step, start, stacked)
    return (outputs.reshape(TOKENS, D), input_grad.reshape(TOKENS, D), totals[0], totals[1], totals[2], totals[3], totals[4], totals[5], totals[6], totals[7], totals[8], totals[9], totals[10], totals[11], totals[12])
```

```python
import functools
import math

import jax
import jax.numpy as jnp
from jax import lax
from jax.experimental import pallas as pl
from jax.experimental.pallas import tpu as pltpu
from jax.sharding import PartitionSpec as P

D = 1152
HD = 72
SEQ = 256


EPS = 1e-06
CUBIC = 0.044715
ROOT = math.sqrt(2.0 / math.pi)


def outer_sum(left, right):
    return lax.dot_general(
        left, right, (((0,), (0,)), ((), ())), preferred_element_type=jnp.float32
    )


def times_transpose(left, right):
    return lax.dot_general(
        left, right, (((1,), (1,)), ((), ())), preferred_element_type=jnp.float32
    )


def row_sums(first, second):
    return lax.psum((first, second), "emb")


def normalize(inputs, gain_row, shift_row):
    totals, squares = row_sums(jnp.sum(inputs, axis=1), jnp.sum(inputs * inputs, axis=1))
    average = totals[:, None] / D
    variance = squares[:, None] / D - average * average
    inverse = lax.rsqrt(variance + EPS)
    centered = (inputs - average) * inverse
    return (centered, inverse, (centered * gain_row + shift_row).astype(jnp.bfloat16))


def norm_back(normed_grad, centered, inverse, gain_row):
    scaled = normed_grad * gain_row
    first, second = row_sums(jnp.sum(scaled, axis=1), jnp.sum(scaled * centered, axis=1))
    return inverse * (scaled - first[:, None] / D - centered * (second[:, None] / D))


def gelu_parts(pre_act):
    inner = ROOT * (pre_act + CUBIC * pre_act * pre_act * pre_act)
    hyper = jnp.tanh(inner)
    values = 0.5 * pre_act * (1.0 + hyper)
    slope = 0.5 * (1.0 + hyper) + 0.5 * pre_act * (1.0 - hyper * hyper) * ROOT * (
        1.0 + 3.0 * CUBIC * pre_act * pre_act
    )
    return (values, slope)


def spread_rows(normed):
    return lax.all_gather(normed, "mdl", axis=0, tiled=True)


def width_sums(gathered, weight, own_rows):

    def partial_rows(first_row, row_count):
        return jnp.dot(gathered, weight, preferred_element_type=jnp.float32)

    return lax.psum_scatter(
        partial_rows(jnp.int32(0), own_rows * lax.axis_size("emb")),
        "emb",
        scatter_dimension=0,
        tiled=True,
    )


def spread_halves(branch):
    return lax.all_gather(branch, "emb", axis=0, tiled=True)


def token_sums(gathered, weight, own_rows):

    def partial_rows(first_row, row_count):
        return jnp.dot(gathered, weight, preferred_element_type=jnp.float32)

    return lax.psum_scatter(
        partial_rows(jnp.int32(0), own_rows * lax.axis_size("mdl")),
        "mdl",
        scatter_dimension=0,
        tiled=True,
    )


def spread_grads(grad_rows):
    return lax.all_gather(grad_rows, "mdl", axis=0, tiled=True)


def grad_width_sums(gathered, weight, own_rows):

    def partial_rows(first_row, row_count):
        return times_transpose(gathered, weight)

    return lax.psum_scatter(
        partial_rows(jnp.int32(0), own_rows * lax.axis_size("emb")),
        "emb",
        scatter_dimension=0,
        tiled=True,
    )


def spread_branch_grads(grad_rows):
    return lax.all_gather(grad_rows, "emb", axis=0, tiled=True)


def grad_token_sums(gathered, weight, own_rows):

    def partial_rows(first_row, row_count):
        return times_transpose(gathered, weight)

    return lax.psum_scatter(
        partial_rows(jnp.int32(0), own_rows * lax.axis_size("mdl")),
        "mdl",
        scatter_dimension=0,
        tiled=True,
    )


def attend(qkv):
    queries = qkv[:, :, :, 0]
    key_rows = qkv[:, :, :, 1]
    value_rows = qkv[:, :, :, 2]
    factor = 1.0 / math.sqrt(HD)
    scores = (
        jnp.einsum("bqhd,bkhd->bhqk", queries, key_rows, preferred_element_type=jnp.float32)
        * factor
    )
    highest = jnp.max(scores, axis=3, keepdims=True)
    log_total = highest + jnp.log(jnp.sum(jnp.exp(scores - highest), axis=3, keepdims=True))
    chances = jnp.exp(scores - log_total).astype(jnp.bfloat16)
    attended = jnp.einsum(
        "bhqk,bkhd->bqhd", chances, value_rows, preferred_element_type=jnp.float32
    ).astype(jnp.bfloat16)
    return (attended, log_total)


def attend_back(qkv, attended, log_total, attended_grad):
    queries = qkv[:, :, :, 0]
    key_rows = qkv[:, :, :, 1]
    value_rows = qkv[:, :, :, 2]
    factor = 1.0 / math.sqrt(HD)
    scores = (
        jnp.einsum("bqhd,bkhd->bhqk", queries, key_rows, preferred_element_type=jnp.float32)
        * factor
    )
    chances = jnp.exp(scores - log_total)
    value_grad = jnp.einsum(
        "bhqk,bqhd->bkhd",
        chances.astype(jnp.bfloat16),
        attended_grad,
        preferred_element_type=jnp.float32,
    ).astype(jnp.bfloat16)
    chance_grad = jnp.einsum(
        "bqhd,bkhd->bhqk", attended_grad, value_rows, preferred_element_type=jnp.float32
    )
    row_dot = jnp.einsum(
        "bqhd,bqhd->bhq", attended_grad, attended, preferred_element_type=jnp.float32
    )[..., None]
    score_grad = (chances * (chance_grad - row_dot)).astype(jnp.bfloat16)
    query_grad = (
        jnp.einsum("bhqk,bkhd->bqhd", score_grad, key_rows, preferred_element_type=jnp.float32)
        * factor
    ).astype(jnp.bfloat16)
    key_grad = (
        jnp.einsum("bhqk,bqhd->bkhd", score_grad, queries, preferred_element_type=jnp.float32)
        * factor
    ).astype(jnp.bfloat16)
    return jnp.stack([query_grad, key_grad, value_grad], axis=3)


def per_device(
    inputs,
    norm1_gain,
    norm1_shift,
    qkv_weight,
    query_bias,
    value_bias,
    out_weight,
    out_bias,
    norm2_gain,
    norm2_shift,
    fc1_weight,
    fc1_bias,
    fc2_weight,
    fc2_bias,
    cotangent,
):
    rows_model = inputs.shape[0]
    group_rows = rows_model * lax.axis_size("mdl")
    half_rows = group_rows // lax.axis_size("emb")
    images_here = half_rows // SEQ
    heads_here = query_bias.shape[0] // HD
    bias_local = jnp.stack(
        [
            query_bias.reshape(heads_here, HD),
            jnp.zeros((heads_here, HD), jnp.float32),
            value_bias.reshape(heads_here, HD),
        ],
        axis=1,
    )
    centered1, inverse1, normed1 = normalize(inputs, norm1_gain, norm1_shift)
    gathered1 = spread_rows(normed1)
    mixed = (
        width_sums(gathered1, qkv_weight, half_rows).reshape(images_here, SEQ, heads_here, 3, HD)
        + bias_local
    )
    qkv = mixed.astype(jnp.bfloat16)
    attended, log_total = attend(qkv)
    attended_rows = spread_halves(attended.reshape(half_rows, heads_here * HD))
    middle = inputs + token_sums(attended_rows, out_weight, rows_model) + out_bias
    centered2, inverse2, normed2 = normalize(middle, norm2_gain, norm2_shift)
    gathered2 = spread_rows(normed2)
    pre_act = width_sums(gathered2, fc1_weight, half_rows) + fc1_bias
    act_values, slope = gelu_parts(pre_act)
    act_rows = spread_halves(act_values.astype(jnp.bfloat16))
    outputs = middle + token_sums(act_rows, fc2_weight, rows_model) + fc2_bias
    cot_rows = spread_grads(cotangent.astype(jnp.bfloat16))
    fc2_weight_grad = outer_sum(act_rows, cot_rows)
    fc2_bias_grad = jnp.sum(cotangent, axis=0)
    pre_grad = (grad_width_sums(cot_rows, fc2_weight, half_rows) * slope).astype(jnp.bfloat16)
    pre_rows = spread_branch_grads(pre_grad)
    fc1_weight_grad = outer_sum(gathered2, pre_rows)
    fc1_bias_grad = jnp.sum(pre_rows.astype(jnp.float32), axis=0)
    normed2_grad = grad_token_sums(pre_rows, fc1_weight, rows_model)
    norm2_gain_grad = jnp.sum(normed2_grad * centered2, axis=0)
    norm2_shift_grad = jnp.sum(normed2_grad, axis=0)
    middle_grad = cotangent + norm_back(normed2_grad, centered2, inverse2, norm2_gain)
    out_bias_grad = jnp.sum(middle_grad, axis=0)
    middle_rows = spread_grads(middle_grad.astype(jnp.bfloat16))
    out_weight_grad = outer_sum(attended_rows, middle_rows)
    attended_grad = (
        grad_width_sums(middle_rows, out_weight, half_rows)
        .astype(jnp.bfloat16)
        .reshape(images_here, SEQ, heads_here, HD)
    )
    qkv_grad = attend_back(qkv, attended, log_total, attended_grad).reshape(
        half_rows, heads_here * 3 * HD
    )
    qkv_rows = spread_branch_grads(qkv_grad)
    qkv_weight_grad = outer_sum(gathered1, qkv_rows)
    column_sums = jnp.sum(qkv_rows.astype(jnp.float32), axis=0).reshape(heads_here, 3, HD)
    query_bias_grad = column_sums[:, 0].reshape(heads_here * HD)
    value_bias_grad = column_sums[:, 2].reshape(heads_here * HD)
    normed1_grad = grad_token_sums(qkv_rows, qkv_weight, rows_model)
    norm1_gain_grad = jnp.sum(normed1_grad * centered1, axis=0)
    norm1_shift_grad = jnp.sum(normed1_grad, axis=0)
    input_grad = middle_grad + norm_back(normed1_grad, centered1, inverse1, norm1_gain)
    (
        qkv_weight_grad,
        query_bias_grad,
        value_bias_grad,
        out_weight_grad,
        fc1_weight_grad,
        fc1_bias_grad,
        fc2_weight_grad,
    ) = lax.psum(
        (
            qkv_weight_grad,
            query_bias_grad,
            value_bias_grad,
            out_weight_grad,
            fc1_weight_grad,
            fc1_bias_grad,
            fc2_weight_grad,
        ),
        "dp",
    )
    (
        out_bias_grad,
        fc2_bias_grad,
        norm1_gain_grad,
        norm1_shift_grad,
        norm2_gain_grad,
        norm2_shift_grad,
    ) = lax.psum(
        (
            out_bias_grad,
            fc2_bias_grad,
            norm1_gain_grad,
            norm1_shift_grad,
            norm2_gain_grad,
            norm2_shift_grad,
        ),
        ("dp", "mdl"),
    )
    return (
        outputs,
        input_grad,
        norm1_gain_grad,
        norm1_shift_grad,
        qkv_weight_grad,
        query_bias_grad,
        value_bias_grad,
        out_weight_grad,
        out_bias_grad,
        norm2_gain_grad,
        norm2_shift_grad,
        fc1_weight_grad,
        fc1_bias_grad,
        fc2_weight_grad,
        fc2_bias_grad,
    )


PARAMS = pltpu.CompilerParams(vmem_limit_bytes=56 * 1024 * 1024)


def mm(left, right):
    return lax.dot_general(
        left, right, (((1,), (0,)), ((), ())), preferred_element_type=jnp.float32
    )


def stats(rows):
    lo, hi = rows
    total = jnp.sum(lo, axis=1, keepdims=True) + jnp.sum(hi, axis=1, keepdims=True)
    square = jnp.sum(lo * lo, axis=1, keepdims=True) + jnp.sum(hi * hi, axis=1, keepdims=True)
    average = total / D
    variance = square / D - average * average
    inverse = lax.rsqrt(variance + EPS)
    return ((lo - average) * inverse, (hi - average) * inverse), inverse


def call(kernel, outs, *args, smem=1):
    specs = [pl.BlockSpec(memory_space=pltpu.SMEM)] * smem
    specs += [pl.BlockSpec(memory_space=pltpu.VMEM)] * (len(args) - smem)
    return pl.pallas_call(
        kernel,
        out_shape=[jax.ShapeDtypeStruct(s, d) for s, d in outs],
        in_specs=specs,
        out_specs=[pl.BlockSpec(memory_space=pltpu.VMEM)] * len(outs),
        compiler_params=PARAMS,
    )(*args)


def four(refs, half):
    a, b, c, d = (r[half].astype(jnp.float32) for r in refs)
    return (a + b) + (c + d)


def norm1_kernel(ids, own, recv, gain, shift, full, normed):
    e = ids[0]
    full[e] = own[...]
    full[1 - e] = recv[...]
    centered, _ = stats((full[0], full[1]))
    for h in range(2):
        normed[h] = (centered[h] * gain[h] + shift[h]).astype(jnp.bfloat16)


def cot_kernel(ids, own, recv, full, low, bias_grad):
    e = ids[0]
    full[e] = own[...]
    full[1 - e] = recv[...]
    for h in range(2):
        low[h] = full[h].astype(jnp.bfloat16)
        bias_grad[h] = jnp.sum(full[h], axis=0, keepdims=True)


def norm2_kernel(full, r1, r2, r3, r4, bias, gain, shift, middle, normed):
    for h in range(2):
        middle[h] = full[h] + four((r1, r2, r3, r4), h) + bias[h]
    centered, _ = stats((middle[0], middle[1]))
    for h in range(2):
        normed[h] = (centered[h] * gain[h] + shift[h]).astype(jnp.bfloat16)


def back_rows(normed_grad, rows, gain, base):
    centered, inverse = stats(rows)
    scaled = [normed_grad[h] * gain[h] for h in range(2)]
    first = sum(jnp.sum(scaled[h], axis=1, keepdims=True) for h in range(2)) / D
    second = (
        sum(jnp.sum(scaled[h] * centered[h], axis=1, keepdims=True) for h in range(2)) / D
    )
    result = [
        base[h] + inverse * (scaled[h] - first - centered[h] * second) for h in range(2)
    ]
    return result, centered


def norm2_back_kernel(
    middle, r1, r2, r3, r4, cot, gain, grad, low, gain_grad, shift_grad, bias_grad
):
    normed_grad = [four((r1, r2, r3, r4), h) for h in range(2)]
    result, centered = back_rows(
        normed_grad, (middle[0], middle[1]), gain, (cot[0], cot[1])
    )
    for h in range(2):
        grad[h] = result[h]
        low[h] = result[h].astype(jnp.bfloat16)
        gain_grad[h] = jnp.sum(normed_grad[h] * centered[h], axis=0, keepdims=True)
        shift_grad[h] = jnp.sum(normed_grad[h], axis=0, keepdims=True)
        bias_grad[h] = jnp.sum(result[h], axis=0, keepdims=True)


def norm1_back_kernel(
    ids, full, r1, r2, r3, r4, base, gain, own, send, gain_grad, shift_grad
):
    e = ids[0]
    normed_grad = [four((r1, r2, r3, r4), h) for h in range(2)]
    result, centered = back_rows(normed_grad, (full[0], full[1]), gain, (base[0], base[1]))
    own[...] = jnp.where(e == 0, result[0], result[1])
    send[...] = jnp.where(e == 0, result[1], result[0])
    for h in range(2):
        gain_grad[h] = jnp.sum(normed_grad[h] * centered[h], axis=0, keepdims=True)
        shift_grad[h] = jnp.sum(normed_grad[h], axis=0, keepdims=True)


def output_kernel(ids, middle, r1, r2, r3, r4, bias, own, send):
    e = ids[0]
    refs = (r1, r2, r3, r4)
    own[...] = middle[e] + four(refs, e) + bias[e]
    send[...] = middle[1 - e] + four(refs, 1 - e) + bias[1 - e]


def join_kernel(ids, own, recv, full):
    e = ids[0]
    full[e] = own[...]
    full[1 - e] = recv[...]


def image(one, two, half):
    return jnp.concatenate([one[half], two[half]], axis=0)


def attend_kernel(
    ids, x1, x2, w_own, w_oth, bias, wo_own, wo_oth, qkv_out, att_out, log_out, o1, o2
):
    e = ids[0]
    heads = att_out.shape[1] // HD
    mixed = mm(image(x1, x2, e), w_own[...]) + mm(image(x1, x2, 1 - e), w_oth[...])
    qkv = (mixed + bias[...]).astype(jnp.bfloat16)
    qkv_out[...] = qkv
    factor = 1.0 / math.sqrt(HD)
    for h in range(heads):
        q, k, v = (qkv[:, (3 * h + j) * HD : (3 * h + j + 1) * HD] for j in range(3))
        scores = times_transpose(q, k) * factor
        highest = jnp.max(scores, axis=1, keepdims=True)
        raised = jnp.exp(scores - highest)
        total = jnp.sum(raised, axis=1, keepdims=True)
        log_out[:, h : h + 1] = highest + jnp.log(total)
        chances = (raised * (1.0 / total)).astype(jnp.bfloat16)
        att_out[:, h * HD : (h + 1) * HD] = mm(chances, v).astype(jnp.bfloat16)
    att = att_out[...]
    for half, weight in ((e, wo_own), (1 - e, wo_oth)):
        part = mm(att, weight[...]).astype(jnp.bfloat16)
        o1[half] = part[: part.shape[0] // 2]
        o2[half] = part[part.shape[0] // 2 :]


def mlp_kernel(
    ids, x1, x2, c1, c2, w1_own, w1_oth, bias, w2_own, w2_oth,
    act_out, pre_out, bias_grad, y1, y2, g1, g2,
):
    e = ids[0]
    pre_act = mm(image(x1, x2, e), w1_own[...]) + mm(image(x1, x2, 1 - e), w1_oth[...])
    values, slope = gelu_parts(pre_act + bias[...])
    act = values.astype(jnp.bfloat16)
    act_out[...] = act
    back = times_transpose(image(c1, c2, e), w2_own[...]) + times_transpose(
        image(c1, c2, 1 - e), w2_oth[...]
    )
    pre_grad = (back * slope).astype(jnp.bfloat16)
    pre_out[...] = pre_grad
    bias_grad[...] = jnp.sum(pre_grad.astype(jnp.float32), axis=0, keepdims=True)
    for half, weight in ((e, w1_own), (1 - e, w1_oth)):
        part = times_transpose(pre_grad, weight[...]).astype(jnp.bfloat16)
        g1[half] = part[: part.shape[0] // 2]
        g2[half] = part[part.shape[0] // 2 :]
    for half, weight in ((e, w2_own), (1 - e, w2_oth)):
        part = mm(act, weight[...]).astype(jnp.bfloat16)
        y1[half] = part[: part.shape[0] // 2]
        y2[half] = part[part.shape[0] // 2 :]


def attend_back_kernel(
    ids, m1, m2, qkv_ref, att_ref, log_ref, wo_own, wo_oth, w_own, w_oth,
    grad_out, sums, g1, g2,
):
    e = ids[0]
    heads = att_ref.shape[1] // HD
    att_grad = (
        times_transpose(image(m1, m2, e), wo_own[...])
        + times_transpose(image(m1, m2, 1 - e), wo_oth[...])
    ).astype(jnp.bfloat16)
    qkv = qkv_ref[...]
    att = att_ref[...]
    factor = 1.0 / math.sqrt(HD)
    for h in range(heads):
        q, k, v = (qkv[:, (3 * h + j) * HD : (3 * h + j + 1) * HD] for j in range(3))
        grad = att_grad[:, h * HD : (h + 1) * HD]
        out = att[:, h * HD : (h + 1) * HD]
        scores = times_transpose(q, k) * factor
        chances = jnp.exp(scores - log_ref[:, h : h + 1])
        value_grad = outer_sum(chances.astype(jnp.bfloat16), grad)
        chance_grad = times_transpose(grad, v)
        row_dot = jnp.sum(
            grad.astype(jnp.float32) * out.astype(jnp.float32), axis=1, keepdims=True
        )
        score_grad = (chances * (chance_grad - row_dot)).astype(jnp.bfloat16)
        query_grad = mm(score_grad, k) * factor
        key_grad = outer_sum(score_grad, q) * factor
        for j, part in enumerate((query_grad, key_grad, value_grad)):
            grad_out[:, (3 * h + j) * HD : (3 * h + j + 1) * HD] = part.astype(jnp.bfloat16)
    qkv_grad = grad_out[...]
    sums[...] = jnp.sum(qkv_grad.astype(jnp.float32), axis=0, keepdims=True)
    for half, weight in ((e, w_own), (1 - e, w_oth)):
        part = times_transpose(qkv_grad, weight[...]).astype(jnp.bfloat16)
        g1[half] = part[: part.shape[0] // 2]
        g2[half] = part[part.shape[0] // 2 :]


def token_outer(half, blocks, parts, swapped):
    total = None
    for i, part in enumerate(parts):
        rows = image(blocks[2 * i], blocks[2 * i + 1], half)
        term = outer_sum(part[...], rows) if swapped else outer_sum(rows, part[...])
        total = term if total is None else total + term
    return total


def weight_send_kernel(swapped, ids, b1, b2, b3, b4, p1, p2, send):
    send[...] = token_outer(1 - ids[0], (b1, b2, b3, b4), (p1, p2), swapped).astype(
        jnp.bfloat16
    )


def weight_own_kernel(
    swapped, ids, b1, b2, b3, b4, p1, p2, recv, own, s1, s2, s3, whole
):
    rows = whole.shape[0]
    quarter = own.shape[0]
    whole[...] = token_outer(ids[0], (b1, b2, b3, b4), (p1, p2), swapped) + recv[...].astype(
        jnp.float32
    )
    rest = rows - 3 * quarter
    for k, target in enumerate((own, s1, s2, s3)):
        index = ids[1] ^ k

        def store(first, count, target=target):
            target[:count, :] = whole[pl.ds(first, count), :].astype(target.dtype)

        if rest == quarter:
            store(pl.multiple_of(index * quarter, 8), quarter)
        else:

            @pl.when(index < 3)
            def _(index=index, store=store):
                store(pl.multiple_of(index * quarter, 8), quarter)

            @pl.when(index == 3)
            def _(store=store, target=target):
                store(3 * quarter, rest)
                target[rest:, :] = jnp.zeros((quarter - rest, target.shape[1]), target.dtype)


def quarter_sum_kernel(own, r1, r2, r3, out):
    out[...] = (
        (own[...] + r1[...].astype(jnp.float32))
        + (r2[...].astype(jnp.float32) + r3[...].astype(jnp.float32))
    ).astype(jnp.bfloat16)


def quarter_join_kernel(ids, u0, u1, u2, u3, out):
    rows = out.shape[0]
    quarter = u0.shape[0]
    rest = rows - 3 * quarter
    for k, part in enumerate((u0, u1, u2, u3)):
        index = ids[1] ^ k
        if rest == quarter:
            out[pl.ds(pl.multiple_of(index * quarter, 8), quarter), :] = part[...].astype(
                jnp.float32
            )
        else:

            @pl.when(index < 3)
            def _(index=index, part=part):
                out[pl.ds(pl.multiple_of(index * quarter, 8), quarter), :] = part[
                    ...
                ].astype(jnp.float32)

            @pl.when(index == 3)
            def _(part=part):
                out[3 * quarter :, :] = part[:rest].astype(jnp.float32)


GROUP = ("mdl", "emb")


def place(z, core):
    return (z % 4) * 2 + core


MOVES = (
    [(place(z, 1), place(z, 0)) for z in range(4)]
    + [(place(z, 0), place(z + 1, 1)) for z in range(4)],
    [(place(z, 0), place(z, 0)) for z in range(4)]
    + [(place(z, 1), place(z + 1, 1)) for z in range(4)],
    [(place(z, 0), place(z + 2, 0)) for z in range(4)]
    + [(place(z, 1), place(z - 1, 1)) for z in range(4)],
    [(place(z, 1), place(z + 2, 0)) for z in range(4)]
    + [(place(z, 0), place(z - 1, 1)) for z in range(4)],
)
BACKS = tuple([(b, a) for a, b in move] for move in MOVES)
SWAP = [(0, 1), (1, 0)]


def flips(count):
    return [[(i, i ^ k) for i in range(count)] for k in range(1, count)]


def spread(block):
    return tuple(lax.ppermute(block, GROUP, move) for move in MOVES)


def collect(parts):
    return tuple(lax.ppermute(p, GROUP, back) for p, back in zip(parts, BACKS))


def swap(value):
    return lax.ppermute(value, "emb", SWAP)


def fast_device(
    inputs,
    norm1_gain,
    norm1_shift,
    qkv_weight,
    query_bias,
    value_bias,
    out_weight,
    out_bias,
    norm2_gain,
    norm2_shift,
    fc1_weight,
    fc1_bias,
    fc2_weight,
    fc2_bias,
    cotangent,
):
    f32, b16 = jnp.float32, jnp.bfloat16
    rows, width = inputs.shape
    half = rows // 2
    heads = query_bias.shape[0] // HD
    e = lax.axis_index("emb")
    dp = lax.axis_index("dp")
    ids = jnp.stack([e, dp]).astype(jnp.int32)
    block = (2, half, width)
    vec = (2, 1, width)

    def parts_of(value):
        own = lax.dynamic_slice_in_dim(value, e * half, half, 0)
        other = lax.dynamic_slice_in_dim(value, (1 - e) * half, half, 0)
        return own, swap(other)

    in_own, in_recv = parts_of(inputs)
    vectors = jnp.stack(
        [norm1_gain, norm1_shift, out_bias, norm2_gain, norm2_shift, fc2_bias]
    )
    vectors_recv = swap(vectors)
    vectors = jnp.where(
        e == 0,
        jnp.stack([vectors, vectors_recv], 1),
        jnp.stack([vectors_recv, vectors], 1),
    )[:, :, None, :]
    gain1, shift1, bias_out, gain2, shift2, bias_fc2 = (vectors[i] for i in range(6))
    full, normed1 = call(
        norm1_kernel, [(block, f32), (block, b16)], ids, in_own, in_recv, gain1, shift1
    )
    xs = spread(normed1)
    qkv_oth = swap(qkv_weight)
    out_oth = swap(out_weight)
    cot_own, cot_recv = parts_of(cotangent)
    cot, cot_low, fc2_bias_grad = call(
        cot_kernel, [(block, f32), (block, b16), (vec, f32)], ids, cot_own, cot_recv
    )
    fc1_oth = swap(fc1_weight)
    fc2_oth = swap(fc2_weight)
    qkv_bias = jnp.stack(
        [
            query_bias.reshape(heads, HD),
            jnp.zeros((heads, HD), f32),
            value_bias.reshape(heads, HD),
        ],
        axis=1,
    ).reshape(1, heads * 3 * HD)

    def pairs(values):
        return (values[0], values[1]), (values[2], values[3])

    qkvs, atts, logs, backs = [], [], [], []
    for x in pairs(xs):
        qkv, att, log, o1, o2 = call(
            attend_kernel,
            [
                ((rows, heads * 3 * HD), b16),
                ((rows, heads * HD), b16),
                ((rows, heads), f32),
                (block, b16),
                (block, b16),
            ],
            ids, *x, qkv_weight, qkv_oth, qkv_bias, out_weight, out_oth,
        )
        qkvs.append(qkv)
        atts.append(att)
        logs.append(log)
        backs += [o1, o2]
    cs = spread(cot_low)
    middle, normed2 = call(
        norm2_kernel, [(block, f32), (block, b16)],
        full, *collect(backs), bias_out, gain2, shift2, smem=0,
    )
    ns = spread(normed2)
    hidden = fc1_bias.shape[0]
    acts, pres, pre_sums, ys, gs = [], [], [], [], []
    for x, c in zip(pairs(ns), pairs(cs)):
        act, pre, pre_sum, y1, y2, g1, g2 = call(
            mlp_kernel,
            [((rows, hidden), b16)] * 2 + [((1, hidden), f32)] + [(block, b16)] * 4,
            ids, *x, *c, fc1_weight, fc1_oth, fc1_bias.reshape(1, hidden),
            fc2_weight, fc2_oth,
        )
        acts.append(act)
        pres.append(pre)
        pre_sums.append(pre_sum)
        ys += [y1, y2]
        gs += [g1, g2]
    middle_grad, mid_low, gain2_grad, shift2_grad, bias_out_grad = call(
        norm2_back_kernel,
        [(block, f32), (block, b16)] + [(vec, f32)] * 3,
        middle, *collect(gs), cot, gain2, smem=0,
    )
    ms = spread(mid_low)
    out_own, out_send = call(
        output_kernel, [((half, width), f32)] * 2,
        ids, middle, *collect(ys), bias_fc2,
    )
    outputs = call(join_kernel, [(block, f32)], ids, out_own, swap(out_send))[0].reshape(
        rows, width
    )

    def weight_grad(shape, blocks, parts, swapped):
        quarter = -(-shape[0] // 32) * 8
        recv = swap(
            call(
                functools.partial(weight_send_kernel, swapped), [(shape, b16)],
                ids, *blocks, *parts,
            )[0]
        )
        sends = [((quarter, shape[1]), f32)] + [((quarter, shape[1]), b16)] * 3
        own, *sends = pl.pallas_call(
            functools.partial(weight_own_kernel, swapped),
            out_shape=[jax.ShapeDtypeStruct(s, d) for s, d in sends],
            in_specs=[pl.BlockSpec(memory_space=pltpu.SMEM)]
            + [pl.BlockSpec(memory_space=pltpu.VMEM)] * 7,
            out_specs=[pl.BlockSpec(memory_space=pltpu.VMEM)] * 4,
            scratch_shapes=[pltpu.VMEM(shape, f32)],
            compiler_params=PARAMS,
        )(ids, *blocks, *parts, recv)
        moves = flips(4)
        recvs = [lax.ppermute(s, "dp", m) for s, m in zip(sends, moves)]
        total = call(
            quarter_sum_kernel, [((quarter, shape[1]), b16)], own, *recvs, smem=0
        )[0]
        others = [lax.ppermute(total, "dp", m) for m in moves]
        return call(quarter_join_kernel, [(shape, f32)], ids, total, *others)[0]

    fc2_weight_grad = weight_grad(fc2_weight.shape, cs, acts, True)
    fc1_weight_grad = weight_grad(fc1_weight.shape, ns, pres, False)

    grads, grad_sums, gs = [], [], []
    for m, qkv, att, log in zip(pairs(ms), qkvs, atts, logs):
        grad, sums, g1, g2 = call(
            attend_back_kernel,
            [((rows, heads * 3 * HD), b16), ((1, heads * 3 * HD), f32)] + [(block, b16)] * 2,
            ids, *m, qkv, att, log, out_weight, out_oth, qkv_weight, qkv_oth,
        )
        grads.append(grad)
        grad_sums.append(sums)
        gs += [g1, g2]
    out_weight_grad = weight_grad(out_weight.shape, ms, atts, True)
    qkv_weight_grad = weight_grad(qkv_weight.shape, xs, grads, False)
    in_own, in_send, gain1_grad, shift1_grad = call(
        norm1_back_kernel,
        [((half, width), f32)] * 2 + [(vec, f32)] * 2,
        ids, full, *collect(gs), middle_grad, gain1,
    )
    input_grad = call(join_kernel, [(block, f32)], ids, in_own, swap(in_send))[0].reshape(
        rows, width
    )

    def exchange(value, axis):
        r1, r2, r3 = (lax.ppermute(value, axis, m) for m in flips(4))
        return (value + r1) + (r2 + r3)

    token_part = jnp.concatenate(
        [v.reshape(-1) for v in (bias_out_grad, fc2_bias_grad, gain1_grad, shift1_grad, gain2_grad, shift2_grad)]
    )
    token_part = exchange(token_part, "mdl")
    group_part = jnp.concatenate(
        [(grad_sums[0] + grad_sums[1]).reshape(-1), (pre_sums[0] + pre_sums[1]).reshape(-1)]
    )
    packed = jnp.concatenate([token_part, group_part])
    packed = packed + swap(packed)
    packed = exchange(packed, "dp")
    rowed = packed[: 12 * width].reshape(6, 2, width)
    (
        out_bias_grad,
        fc2_bias_grad,
        norm1_gain_grad,
        norm1_shift_grad,
        norm2_gain_grad,
        norm2_shift_grad,
    ) = (lax.dynamic_index_in_dim(rowed[i], e, 0, False) for i in range(6))
    qkv_sums = packed[12 * width : 12 * width + heads * 3 * HD].reshape(heads, 3, HD)
    fc1_bias_grad = packed[12 * width + heads * 3 * HD :]
    return (
        outputs,
        input_grad,
        norm1_gain_grad,
        norm1_shift_grad,
        qkv_weight_grad,
        qkv_sums[:, 0].reshape(-1),
        qkv_sums[:, 2].reshape(-1),
        out_weight_grad,
        out_bias_grad,
        norm2_gain_grad,
        norm2_shift_grad,
        fc1_weight_grad,
        fc1_bias_grad,
        fc2_weight_grad,
        fc2_bias_grad,
    )


def solution(mesh):
    in_specs = (
        P(("dp", "mdl"), "emb"),
        P("emb"),
        P("emb"),
        P("emb", "mdl"),
        P("mdl"),
        P("mdl"),
        P("mdl", "emb"),
        P("emb"),
        P("emb"),
        P("emb"),
        P("emb", "mdl"),
        P("mdl"),
        P("mdl", "emb"),
        P("emb"),
        P(("dp", "mdl"), "emb"),
    )
    out_specs = (
        P(("dp", "mdl"), "emb"),
        P(("dp", "mdl"), "emb"),
        P("emb"),
        P("emb"),
        P("emb", "mdl"),
        P("mdl"),
        P("mdl"),
        P("mdl", "emb"),
        P("emb"),
        P("emb"),
        P("emb"),
        P("emb", "mdl"),
        P("mdl"),
        P("mdl", "emb"),
        P("emb"),
    )
    sizes = (mesh.shape["dp"], mesh.shape["mdl"], mesh.shape["emb"])

    def program(inputs, *rest):
        fits = sizes == (4, 4, 2) and inputs.shape[0] == 16 * SEQ
        return jax.shard_map(
            fast_device if fits else per_device, mesh=mesh, in_specs=in_specs, out_specs=out_specs, check_vma=False
        )(inputs, *rest)

    return program
```
